32 devices in a mesh: rep: 4 (over y, x), shard: 8 (over z, core).
Axes of the slice: x: 2, y: 2, z: 4, core: 2. Of those that a mesh axis runs over, the one named last changes fastest.
Arguments:
- tokens: bfloat16 [8192, 1024], P(('rep', 'shard')), may hold values from -6 to 6
- cotangent: bfloat16 [8192, 1024], P(('rep', 'shard')), may hold values from -6 to 6
- positions: int32 [8192], P(('rep', 'shard')), may hold values from 0 to 255, as said below
- counts: int32 [32], P(('rep', 'shard')), may hold values from 128 to 256, as said below
- attn_weight: bfloat16 [1024, 3072], P('shard'), may hold values from -0.75 to 0.75
- ffn_weight: bfloat16 [4608, 3, 1024], P('shard'), may hold values from -0.1875 to 0.1875
- gains: bfloat16 [2, 1024], P(None, 'shard'), may hold values from 0.099609375 to 1.8984375
- qk_gains: bfloat16 [2, 64], P(None, 'shard'), as said below
Outputs:
- output: bfloat16 [8192, 1024], P(('rep', 'shard'))
- grad_input: bfloat16 [8192, 1024], P(('rep', 'shard'))
- grad_attn: float32 [1024, 3072], P('shard')
- grad_ffn: float32 [4608, 3, 1024], P('shard')
- grad_gains: float32 [2, 1024], P(None, 'shard')
- grad_qk: float32 [2, 64], P(None, 'shard')
The draws below stay inside these ranges and needn't reach their ends.
Inputs may be any that keep to these rules, and one draw needn't show every extreme that they name: `counts`: one device holds 256 real tokens and another 128 in every draw. `positions`: sequences lie whole inside one device's block of 256 slots, one after another; slots at or past the block's count hold 0. `qk_gains`: positive scales.
All inputs are finite; a program needn't handle non-finite values.
Results may differ from the reference program's by a relative error of at most 0.018.
Values may be sent and summed in bfloat16 or wider, within the bound.
A program may use at most 320 MiB of HBM per device.

```python
import jax
import jax.numpy as jnp
from jax import lax

D = 1024
FF = 4608
QUERY_HEADS = 16
KEY_VALUE_HEADS = 8
HEAD_WIDTH = 64
DEVICE_TOKENS = 256
MIN_TOK = 128
QUERY_FEATURES = 1024
KEY_FEATURES = 512
CW = 3072
RANKS = 32
TOKENS = 8192


def plan_tokens(key):
    base = jax.random.fold_in(key, 17)
    count_key, order_key, start_key = jax.random.split(base, 3)
    counts = jax.random.randint(count_key, (RANKS,), MIN_TOK, DEVICE_TOKENS + 1)
    order = jax.random.permutation(order_key, RANKS)
    counts = jnp.where(order == 0, DEVICE_TOKENS, jnp.where(order == 1, MIN_TOK, counts)).astype(jnp.int32)
    index = jnp.arange(DEVICE_TOKENS, dtype=jnp.int32)[None, :]
    starts = (jax.random.randint(start_key, (RANKS, DEVICE_TOKENS), 0, 64) == 0) | (index == 0)
    begin = lax.cummax(jnp.where(starts, index, 0), axis=1)
    offsets = jnp.where(index < counts[:, None], index - begin, 0)
    return (counts, offsets.reshape(-1).astype(jnp.int32))


def draw_counts(key, part):
    return plan_tokens(key)[0]


def draw_positions(key, part):
    return plan_tokens(key)[1]


def draw_qk_gains(key, part):
    value_rows = jax.random.uniform(key, (2, HEAD_WIDTH), jnp.float32, 0.6, 1.8)
    return value_rows.astype(jnp.bfloat16)


def level_of(rng, dims, pieces, least, high):
    level = 1.0
    for position, blocks in pieces:
        steps = jax.random.uniform(jax.random.fold_in(jax.random.fold_in(rng, 6), position), (blocks,), jnp.float32, least / len(pieces), high / len(pieces))
        level = level * jnp.repeat(jnp.exp(steps), dims[position] // blocks).reshape((-1,) + (1,) * (len(dims) - 1 - position))
    return level


def normal_values(stream_key, shape, scale, reach, shards=(), kind=jnp.bfloat16):
    values = scale * jax.random.normal(stream_key, shape, jnp.float32)
    if shards:
        values = values * level_of(stream_key, shape, shards, -0.22, 0.18)
    return jnp.clip(values, -reach, reach).astype(kind)


def setup_inputs(seed: int = 0) -> dict:
    streams_of = jax.random.split(jax.random.key(seed), 9)
    return {
        "tokens": normal_values(streams_of[0], (TOKENS, D), 1.0, 6.0, ((0, 32),)),
        "cotangent": normal_values(streams_of[1], (TOKENS, D), 1.0, 6.0, ((0, 32),)),
        "positions": draw_positions(jax.random.fold_in(streams_of[8], 71), 0),
        "counts": draw_counts(jax.random.fold_in(streams_of[8], 71), 0),
        "attn_weight": normal_values(streams_of[4], (D, CW), (D // 16) ** -0.5, 0.75, ((0, 8),)),
        "ffn_weight": normal_values(streams_of[5], (FF, 3, D), D ** -0.5, 0.1875, ((0, 8),)),
        "gains": jnp.clip(1.0 + 0.18 * jax.random.normal(streams_of[6], (2, D), jnp.float32), 0.099609375, 1.8984375).astype(jnp.bfloat16),
        "qk_gains": draw_qk_gains(jax.random.fold_in(streams_of[8], 71), 0),
    }


EPS = 1e-05
THETA = 1000000.0

def rope_tables(positions):
    half = HEAD_WIDTH // 2
    freq = THETA ** (-2.0 * jnp.arange(half, dtype=jnp.float32) / HEAD_WIDTH)
    angle = positions.astype(jnp.float32)[:, None] * freq[None, :]
    return (jnp.cos(angle), jnp.sin(angle))

def apply_rotation(vectors, cosine_table, sine_table, sign):
    half = vectors.shape[-1] // 2
    upper = vectors[..., :half]
    lower = vectors[..., half:]
    cos_b = cosine_table[:, None, :]
    sin_b = sine_table[:, None, :] * sign
    return jnp.concatenate([upper * cos_b - lower * sin_b, lower * cos_b + upper * sin_b], axis=-1)

def rms_back(grad_normed, unit, inverse, gain):
    inner = grad_normed * gain
    return inverse * (inner - unit * lax.optimization_barrier(jnp.mean(inner * unit, axis=-1, keepdims=True)))

def one_block(x_rows, cot_rows, pos_rows, count, attn_weight, ffn_weight, gains, qk_gains):
    width = QUERY_FEATURES + 2 * KEY_FEATURES
    replica_group = QUERY_HEADS // KEY_VALUE_HEADS
    scale = HEAD_WIDTH ** (-0.5)
    index = jnp.arange(DEVICE_TOKENS, dtype=jnp.int32)
    valid = (index < count).astype(jnp.float32)[:, None]
    allowed = (index[None, :] <= index[:, None]) & (index[None, :] >= (index - pos_rows)[:, None])
    gain_one = gains[0].astype(jnp.float32)
    gain_two = gains[1].astype(jnp.float32)
    query_gain = qk_gains[0].astype(jnp.float32)
    k_gain = qk_gains[1].astype(jnp.float32)
    w_qkv = attn_weight[:, :width]
    out_proj = attn_weight[:, width:]
    wide = x_rows.astype(jnp.float32)
    inv_one = lax.rsqrt(lax.optimization_barrier(jnp.mean(wide * wide, axis=-1, keepdims=True)) + EPS)
    unit_one = wide * inv_one
    normed_one = (unit_one * gain_one).astype(jnp.bfloat16)
    projected_output = jnp.dot(normed_one, w_qkv, preferred_element_type=jnp.float32)
    query = projected_output[:, :QUERY_FEATURES].reshape(DEVICE_TOKENS, QUERY_HEADS, HEAD_WIDTH)
    key_rows = projected_output[:, QUERY_FEATURES:QUERY_FEATURES + KEY_FEATURES].reshape(DEVICE_TOKENS, KEY_VALUE_HEADS, HEAD_WIDTH)
    value_rows = projected_output[:, QUERY_FEATURES + KEY_FEATURES:].reshape(DEVICE_TOKENS, KEY_VALUE_HEADS, HEAD_WIDTH).astype(jnp.bfloat16)
    q_inv = lax.rsqrt(lax.optimization_barrier(jnp.mean(query * query, axis=-1, keepdims=True)) + EPS)
    query_unit = query * q_inv
    k_inv = lax.rsqrt(lax.optimization_barrier(jnp.mean(key_rows * key_rows, axis=-1, keepdims=True)) + EPS)
    k_unit = key_rows * k_inv
    cosine_table, sine_table = rope_tables(pos_rows)
    query_rotated = apply_rotation(query_unit * query_gain, cosine_table, sine_table, 1.0).astype(jnp.bfloat16).reshape(DEVICE_TOKENS, KEY_VALUE_HEADS, replica_group, HEAD_WIDTH)
    key_r = apply_rotation(k_unit * k_gain, cosine_table, sine_table, 1.0).astype(jnp.bfloat16)
    scores = jnp.einsum('qhgd,khd->hgqk', query_rotated.astype(jnp.float32), key_r.astype(jnp.float32)) * scale
    masked = jnp.where(allowed, scores, -1e+30)
    top = lax.optimization_barrier(jnp.max(masked, axis=-1, keepdims=True))
    lse = top + jnp.log(lax.optimization_barrier(jnp.sum(jnp.exp(masked - top), axis=-1, keepdims=True)))
    probs_wide = jnp.exp(masked - lse)
    probs = probs_wide.astype(jnp.bfloat16)
    attended = jnp.einsum('hgqk,khd->qhgd', probs.astype(jnp.float32), value_rows.astype(jnp.float32)).astype(jnp.bfloat16)
    attended_flat = attended.reshape(DEVICE_TOKENS, QUERY_FEATURES)
    mid = wide + jnp.dot(attended_flat, out_proj.T, preferred_element_type=jnp.float32)
    inv_two = lax.rsqrt(lax.optimization_barrier(jnp.mean(mid * mid, axis=-1, keepdims=True)) + EPS)
    unit_two = mid * inv_two
    normed_two = (unit_two * gain_two).astype(jnp.bfloat16)
    gate = jnp.dot(normed_two, ffn_weight[:, 0, :].T, preferred_element_type=jnp.float32)
    up_proj = jnp.dot(normed_two, ffn_weight[:, 1, :].T, preferred_element_type=jnp.float32)
    sig = jax.nn.sigmoid(gate)
    act = gate * sig
    hidden = (act * up_proj).astype(jnp.bfloat16)
    result = ((mid + jnp.dot(hidden, ffn_weight[:, 2, :], preferred_element_type=jnp.float32)) * valid).astype(jnp.bfloat16)
    cot = (cot_rows.astype(jnp.float32) * valid).astype(jnp.bfloat16)
    d_hidden = jnp.dot(cot, ffn_weight[:, 2, :].T, preferred_element_type=jnp.float32)
    d_gate = (d_hidden * up_proj * sig * (1.0 + gate * (1.0 - sig))).astype(jnp.bfloat16)
    d_up = (d_hidden * act).astype(jnp.bfloat16)
    grad_ffn = jnp.stack([jnp.dot(d_gate.T, normed_two, preferred_element_type=jnp.float32), jnp.dot(d_up.T, normed_two, preferred_element_type=jnp.float32), jnp.dot(hidden.T, cot, preferred_element_type=jnp.float32)], axis=1)
    d_normed_two = jnp.dot(d_gate, ffn_weight[:, 0, :], preferred_element_type=jnp.float32) + jnp.dot(d_up, ffn_weight[:, 1, :], preferred_element_type=jnp.float32)
    grad_two = lax.optimization_barrier(jnp.sum(d_normed_two * unit_two, axis=0))
    d_mid = cot.astype(jnp.float32) + rms_back(d_normed_two, unit_two, inv_two, gain_two)
    d_mid_b = d_mid.astype(jnp.bfloat16)
    attended_gradient = jnp.dot(d_mid_b, out_proj, preferred_element_type=jnp.float32).astype(jnp.bfloat16)
    grad_out = jnp.dot(d_mid_b.T, attended_flat, preferred_element_type=jnp.float32)
    attention_gradient = attended_gradient.reshape(DEVICE_TOKENS, KEY_VALUE_HEADS, replica_group, HEAD_WIDTH).astype(jnp.float32)
    d_probs = jnp.einsum('qhgd,khd->hgqk', attention_gradient, value_rows.astype(jnp.float32))
    delta = lax.optimization_barrier(jnp.sum(attention_gradient * attended.astype(jnp.float32), axis=-1))
    delta = jnp.transpose(delta, (1, 2, 0))[..., None]
    d_scores = (probs_wide * (d_probs - delta) * scale).astype(jnp.bfloat16).astype(jnp.float32)
    d_query_r = jnp.einsum('hgqk,khd->qhgd', d_scores, key_r.astype(jnp.float32)).reshape(DEVICE_TOKENS, QUERY_HEADS, HEAD_WIDTH)
    d_key_r = jnp.einsum('hgqk,qhgd->khd', d_scores, query_rotated.astype(jnp.float32))
    d_value = jnp.einsum('hgqk,qhgd->khd', probs.astype(jnp.float32), attention_gradient)
    d_q_scaled = apply_rotation(d_query_r, cosine_table, sine_table, -1.0)
    d_k_scaled = apply_rotation(d_key_r, cosine_table, sine_table, -1.0)
    grad_q = lax.optimization_barrier(jnp.sum(d_q_scaled * query_unit, axis=(0, 1)))
    grad_k = lax.optimization_barrier(jnp.sum(d_k_scaled * k_unit, axis=(0, 1)))
    d_query = rms_back(d_q_scaled, query_unit, q_inv, query_gain)
    d_key = rms_back(d_k_scaled, k_unit, k_inv, k_gain)
    d_projected = jnp.concatenate([d_query.reshape(DEVICE_TOKENS, QUERY_FEATURES), d_key.reshape(DEVICE_TOKENS, KEY_FEATURES), d_value.reshape(DEVICE_TOKENS, KEY_FEATURES)], axis=1).astype(jnp.bfloat16)
    grad_attn = jnp.concatenate([jnp.dot(normed_one.T, d_projected, preferred_element_type=jnp.float32), grad_out], axis=1)
    d_normed_one = jnp.dot(d_projected, w_qkv.T, preferred_element_type=jnp.float32)
    grad_one = lax.optimization_barrier(jnp.sum(d_normed_one * unit_one, axis=0))
    grad_input = (d_mid + rms_back(d_normed_one, unit_one, inv_one, gain_one)).astype(jnp.bfloat16)
    return (result, grad_input, grad_attn, grad_ffn, jnp.stack([grad_one, grad_two]), jnp.stack([grad_q, grad_k]))

def reference(tokens, cotangent, positions, counts, attn_weight, ffn_weight, gains, qk_gains):
    x_all = tokens.reshape(RANKS, DEVICE_TOKENS, D)
    cot_all = cotangent.reshape(RANKS, DEVICE_TOKENS, D)
    pos_all = positions.reshape(RANKS, DEVICE_TOKENS)

    def step_fn(carry, inputs):
        x_rows, cot_rows, pos_rows, count = inputs
        result, grad_input, g_attn, g_ffn, g_gain, g_qk = one_block(x_rows, cot_rows, pos_rows, count, attn_weight, ffn_weight, gains, qk_gains)
        carry = (carry[0] + g_attn, carry[1] + g_ffn, carry[2] + g_gain, carry[3] + g_qk)
        return (carry, (result, grad_input))
    start = (jnp.zeros((D, CW), jnp.float32), jnp.zeros((FF, 3, D), jnp.float32), jnp.zeros((2, D), jnp.float32), jnp.zeros((2, HEAD_WIDTH), jnp.float32))
    sums, outs = lax.scan(step_fn, start, (x_all, cot_all, pos_all, counts))
    return (outs[0].reshape(TOKENS, D), outs[1].reshape(TOKENS, D), sums[0], sums[1], sums[2], sums[3])
```

```python
import jax
import jax.numpy as jnp
from jax import lax
from jax.sharding import PartitionSpec as P

QUERY_HEADS = 16
KEY_VALUE_HEADS = 8
HEAD_WIDTH = 64
QUERY_FEATURES = 1024
KEY_FEATURES = 512


EPS = 1e-05
THETA = 1000000.0
CHUNKS = 2
BOTH = ("rep", "shard")


def rope_tables(positions, head_size):
    half = head_size // 2
    freq = THETA ** (-2.0 * jnp.arange(half, dtype=jnp.float32) / head_size)
    angle = positions.astype(jnp.float32)[:, None] * freq[None, :]
    return (jnp.cos(angle), jnp.sin(angle))


def apply_rotation(vectors, cosine_table, sine_table, sign):
    half = vectors.shape[-1] // 2
    upper = vectors[..., :half]
    lower = vectors[..., half:]
    cos_b = cosine_table[:, None, :]
    sin_b = sine_table[:, None, :] * sign
    return jnp.concatenate([upper * cos_b - lower * sin_b, lower * cos_b + upper * sin_b], axis=-1)


def rms_back(grad_normed, unit, inverse, gain):
    inner = grad_normed * gain
    return inverse * (inner - unit * jnp.mean(inner * unit, axis=-1, keepdims=True))


def times_trans(left, right):
    return lax.dot_general(
        left, right, (((1,), (1,)), ((), ())), preferred_element_type=jnp.float32
    )


def trans_times(left, right):
    return lax.dot_general(
        left, right, (((0,), (0,)), ((), ())), preferred_element_type=jnp.float32
    )


def local(tokens, cotangent, positions, counts, attn_weight, ffn_weight, gains, qk_gains):
    token_rows = tokens.shape[0]
    width = QUERY_FEATURES + 2 * KEY_FEATURES
    replica_group = QUERY_HEADS // KEY_VALUE_HEADS
    scale = HEAD_WIDTH ** (-0.5)
    reps, shards = lax.axis_size("rep"), lax.axis_size("shard")
    group, member = lax.axis_index("rep"), lax.axis_index("shard")
    attn_rows = attn_weight.shape[0] // reps
    attn_cols = attn_weight.shape[1]
    full_attn = lax.all_gather(
        lax.dynamic_slice_in_dim(attn_weight, group * attn_rows, attn_rows, 0), BOTH, axis=0
    )
    full_attn = (
        full_attn.reshape(reps, shards, attn_rows, attn_cols)
        .transpose(1, 0, 2, 3)
        .reshape(-1, attn_cols)
    )
    gain_cols, qk_cols = gains.shape[1], qk_gains.shape[1]
    scales = lax.all_gather(jnp.concatenate([gains, qk_gains], axis=1), "shard", axis=1)
    full_gains = scales[:, :, :gain_cols].reshape(2, -1)
    full_qk = scales[:, :, gain_cols:].reshape(2, -1)
    ffn_rows = ffn_weight.shape[0] // reps // CHUNKS
    pieces = [
        lax.all_gather(
            lax.dynamic_slice_in_dim(ffn_weight, (group * CHUNKS + c) * ffn_rows, ffn_rows, 0),
            BOTH,
            axis=0,
            tiled=True,
        )
        for c in range(CHUNKS)
    ]
    index = jnp.arange(token_rows, dtype=jnp.int32)
    valid = (index < counts[0]).astype(jnp.float32)[:, None]
    allowed = (index[None, :] <= index[:, None]) & (index[None, :] >= (index - positions)[:, None])
    gain_one = full_gains[0].astype(jnp.float32)
    gain_two = full_gains[1].astype(jnp.float32)
    query_gain = full_qk[0].astype(jnp.float32)
    k_gain = full_qk[1].astype(jnp.float32)
    wide = tokens.astype(jnp.float32)
    inv_one = lax.rsqrt(jnp.mean(wide * wide, axis=-1, keepdims=True) + EPS)
    unit_one = wide * inv_one
    normed_one = (unit_one * gain_one).astype(jnp.bfloat16)
    projected_output = jnp.dot(normed_one, full_attn[:, :width], preferred_element_type=jnp.float32)
    query = projected_output[:, :QUERY_FEATURES].reshape(token_rows, QUERY_HEADS, HEAD_WIDTH)
    key_rows = projected_output[:, QUERY_FEATURES : QUERY_FEATURES + KEY_FEATURES].reshape(
        token_rows, KEY_VALUE_HEADS, HEAD_WIDTH
    )
    value_rows = (
        projected_output[:, QUERY_FEATURES + KEY_FEATURES :]
        .reshape(token_rows, KEY_VALUE_HEADS, HEAD_WIDTH)
        .astype(jnp.bfloat16)
    )
    q_inv = lax.rsqrt(jnp.mean(query * query, axis=-1, keepdims=True) + EPS)
    query_unit = query * q_inv
    k_inv = lax.rsqrt(jnp.mean(key_rows * key_rows, axis=-1, keepdims=True) + EPS)
    k_unit = key_rows * k_inv
    cosine_table, sine_table = rope_tables(positions, HEAD_WIDTH)
    query_rotated = (
        apply_rotation(query_unit * query_gain, cosine_table, sine_table, 1.0)
        .astype(jnp.bfloat16)
        .reshape(token_rows, KEY_VALUE_HEADS, replica_group, HEAD_WIDTH)
    )
    key_r = apply_rotation(k_unit * k_gain, cosine_table, sine_table, 1.0).astype(jnp.bfloat16)
    scores = (
        jnp.einsum("qhgd,khd->hgqk", query_rotated, key_r, preferred_element_type=jnp.float32)
        * scale
    )
    masked = jnp.where(allowed, scores, -1e30)
    top = jnp.max(masked, axis=-1, keepdims=True)
    lse = top + jnp.log(jnp.sum(jnp.exp(masked - top), axis=-1, keepdims=True))
    probs = jnp.exp(masked - lse).astype(jnp.bfloat16)
    attended = jnp.einsum(
        "hgqk,khd->qhgd", probs, value_rows, preferred_element_type=jnp.float32
    ).astype(jnp.bfloat16)
    attended_flat = attended.reshape(token_rows, QUERY_FEATURES)
    mid = wide + times_trans(attended_flat, full_attn[:, width:])
    inv_two = lax.rsqrt(jnp.mean(mid * mid, axis=-1, keepdims=True) + EPS)
    unit_two = mid * inv_two
    normed_two = (unit_two * gain_two).astype(jnp.bfloat16)
    cot = (cotangent.astype(jnp.float32) * valid).astype(jnp.bfloat16)
    total = 0.0
    d_normed = 0.0
    ffn_terms = []
    for piece in pieces:
        gate = times_trans(normed_two, piece[:, 0, :])
        up_proj = times_trans(normed_two, piece[:, 1, :])
        d_hidden = times_trans(cot, piece[:, 2, :])
        sig = jax.nn.sigmoid(gate)
        act = gate * sig
        hidden_piece = (act * up_proj).astype(jnp.bfloat16)
        d_gate = (d_hidden * up_proj * sig * (1.0 + gate * (1.0 - sig))).astype(jnp.bfloat16)
        d_up = (d_hidden * act).astype(jnp.bfloat16)
        ffn_terms.append(
            lax.psum_scatter(
                jnp.stack(
                    [
                        trans_times(d_gate, normed_two).astype(jnp.bfloat16),
                        trans_times(d_up, normed_two).astype(jnp.bfloat16),
                        trans_times(hidden_piece, cot).astype(jnp.bfloat16),
                    ],
                    axis=1,
                ),
                BOTH,
                scatter_dimension=0,
                tiled=True,
            )
        )
        total = total + jnp.dot(hidden_piece, piece[:, 2, :], preferred_element_type=jnp.float32)
        d_normed = (
            d_normed
            + jnp.dot(d_gate, piece[:, 0, :], preferred_element_type=jnp.float32)
            + jnp.dot(d_up, piece[:, 1, :], preferred_element_type=jnp.float32)
        )
    result = ((mid + total) * valid).astype(jnp.bfloat16)
    grad_ffn = lax.all_gather(
        jnp.concatenate(ffn_terms, axis=0), "rep", axis=0, tiled=True
    ).astype(jnp.float32)
    grad_two = jnp.sum(d_normed * unit_two, axis=0)
    d_mid = cot.astype(jnp.float32) + rms_back(d_normed, unit_two, inv_two, gain_two)
    d_mid_b = d_mid.astype(jnp.bfloat16)
    attended_gradient = jnp.dot(
        d_mid_b, full_attn[:, width:], preferred_element_type=jnp.float32
    ).astype(jnp.bfloat16)
    attention_gradient = attended_gradient.reshape(
        token_rows, KEY_VALUE_HEADS, replica_group, HEAD_WIDTH
    )
    scores_again = (
        jnp.einsum("qhgd,khd->hgqk", query_rotated, key_r, preferred_element_type=jnp.float32)
        * scale
    )
    probs_wide = jnp.exp(jnp.where(allowed, scores_again, -1e30) - lse)
    d_probs = jnp.einsum(
        "qhgd,khd->hgqk", attention_gradient, value_rows, preferred_element_type=jnp.float32
    )
    delta = jnp.sum(attention_gradient.astype(jnp.float32) * attended.astype(jnp.float32), axis=-1)
    delta = jnp.transpose(delta, (1, 2, 0))[..., None]
    d_scores = (probs_wide * (d_probs - delta) * scale).astype(jnp.bfloat16)
    d_query_r = jnp.einsum(
        "hgqk,khd->qhgd", d_scores, key_r, preferred_element_type=jnp.float32
    ).reshape(token_rows, QUERY_HEADS, HEAD_WIDTH)
    d_key_r = jnp.einsum(
        "hgqk,qhgd->khd", d_scores, query_rotated, preferred_element_type=jnp.float32
    )
    d_value = jnp.einsum(
        "hgqk,qhgd->khd", probs, attention_gradient, preferred_element_type=jnp.float32
    )
    d_q_scaled = apply_rotation(d_query_r, cosine_table, sine_table, -1.0)
    d_k_scaled = apply_rotation(d_key_r, cosine_table, sine_table, -1.0)
    grad_q = jnp.sum(d_q_scaled * query_unit, axis=(0, 1))
    grad_k = jnp.sum(d_k_scaled * k_unit, axis=(0, 1))
    d_query = rms_back(d_q_scaled, query_unit, q_inv, query_gain)
    d_key = rms_back(d_k_scaled, k_unit, k_inv, k_gain)
    d_projected = jnp.concatenate(
        [
            d_query.reshape(token_rows, QUERY_FEATURES),
            d_key.reshape(token_rows, KEY_FEATURES),
            d_value.reshape(token_rows, KEY_FEATURES),
        ],
        axis=1,
    ).astype(jnp.bfloat16)
    d_normed_one = times_trans(d_projected, full_attn[:, :width])
    grad_one = jnp.sum(d_normed_one * unit_one, axis=0)
    grad_input = (d_mid + rms_back(d_normed_one, unit_one, inv_one, gain_one)).astype(jnp.bfloat16)
    attn_terms = jnp.concatenate(
        [
            trans_times(normed_one, d_projected).astype(jnp.bfloat16),
            trans_times(d_mid_b, attended_flat).astype(jnp.bfloat16),
        ],
        axis=1,
    )
    attn_terms = (
        attn_terms.reshape(shards, reps, attn_rows, attn_cols)
        .transpose(1, 0, 2, 3)
        .reshape(-1, attn_cols)
    )
    grad_attn = lax.all_gather(
        lax.psum_scatter(attn_terms, BOTH, scatter_dimension=0, tiled=True),
        "rep",
        axis=0,
        tiled=True,
    ).astype(jnp.float32)
    small = lax.psum(
        jnp.concatenate([jnp.stack([grad_one, grad_two]), jnp.stack([grad_q, grad_k])], axis=1),
        BOTH,
    )
    grad_gains = lax.dynamic_slice_in_dim(small, member * gain_cols, gain_cols, 1)
    grad_qk = lax.dynamic_slice_in_dim(small, QUERY_FEATURES + member * qk_cols, qk_cols, 1)
    return (result, grad_input, grad_attn, grad_ffn, grad_gains, grad_qk)


def solution(mesh):
    in_specs = (
        P(("rep", "shard"), None),
        P(("rep", "shard"), None),
        P(("rep", "shard")),
        P(("rep", "shard")),
        P("shard", None),
        P("shard", None, None),
        P(None, "shard"),
        P(None, "shard"),
    )
    out_specs = (
        P(("rep", "shard"), None),
        P(("rep", "shard"), None),
        P("shard", None),
        P("shard", None, None),
        P(None, "shard"),
        P(None, "shard"),
    )
    return jax.shard_map(local, mesh=mesh, in_specs=in_specs, out_specs=out_specs, check_vma=False)
```

```python
import jax
import jax.numpy as jnp
from jax import lax
from jax.sharding import PartitionSpec as P

QUERY_HEADS = 16
KEY_VALUE_HEADS = 8
HEAD_WIDTH = 64
QUERY_FEATURES = 1024
KEY_FEATURES = 512


EPS = 1e-05
THETA = 1000000.0
CHUNKS = 1
BOTH = ("rep", "shard")


def rope_tables(positions, head_size):
    half = head_size // 2
    freq = THETA ** (-2.0 * jnp.arange(half, dtype=jnp.float32) / head_size)
    angle = positions.astype(jnp.float32)[:, None] * freq[None, :]
    return (jnp.cos(angle), jnp.sin(angle))


def apply_rotation(vectors, cosine_table, sine_table, sign):
    half = vectors.shape[-1] // 2
    upper = vectors[..., :half]
    lower = vectors[..., half:]
    cos_b = cosine_table[:, None, :]
    sin_b = sine_table[:, None, :] * sign
    return jnp.concatenate([upper * cos_b - lower * sin_b, lower * cos_b + upper * sin_b], axis=-1)


def rms_back(grad_normed, unit, inverse, gain):
    inner = grad_normed * gain
    return inverse * (inner - unit * jnp.mean(inner * unit, axis=-1, keepdims=True))


def times_trans(left, right):
    return lax.dot_general(
        left, right, (((1,), (1,)), ((), ())), preferred_element_type=jnp.float32
    )


def trans_times(left, right):
    return lax.dot_general(
        left, right, (((0,), (0,)), ((), ())), preferred_element_type=jnp.float32
    )


def swap_cores(array, devices):
    return lax.ppermute(array, BOTH, [(i, i + 1 - 2 * (i % 2)) for i in range(devices)])


def scatter_cores(array, devices):
    groups = [list(range(0, devices, 2)), list(range(1, devices, 2))]
    return lax.psum_scatter(
        array, BOTH, scatter_dimension=0, axis_index_groups=groups, tiled=True
    )


def local(tokens, cotangent, positions, counts, attn_weight, ffn_weight, gains, qk_gains):
    token_rows = tokens.shape[0]
    width = QUERY_FEATURES + 2 * KEY_FEATURES
    replica_group = QUERY_HEADS // KEY_VALUE_HEADS
    scale = HEAD_WIDTH ** (-0.5)
    reps, shards = lax.axis_size("rep"), lax.axis_size("shard")
    group, member = lax.axis_index("rep"), lax.axis_index("shard")
    core = lax.rem(member, 2)
    attn_rows = attn_weight.shape[0] // reps
    attn_cols = attn_weight.shape[1]
    full_attn = lax.all_gather(
        lax.dynamic_slice_in_dim(attn_weight, group * attn_rows, attn_rows, 0), BOTH, axis=0
    )
    full_attn = (
        full_attn.reshape(reps, shards, attn_rows, attn_cols)
        .transpose(1, 0, 2, 3)
        .reshape(-1, attn_cols)
    )
    gain_cols, qk_cols = gains.shape[1], qk_gains.shape[1]
    scales = lax.all_gather(jnp.concatenate([gains, qk_gains], axis=1), "shard", axis=1)
    full_gains = scales[:, :, :gain_cols].reshape(2, -1)
    full_qk = scales[:, :, gain_cols:].reshape(2, -1)
    ffn_rows = ffn_weight.shape[0] // reps // CHUNKS
    pieces = [
        lax.all_gather(
            lax.dynamic_slice_in_dim(ffn_weight, (group * CHUNKS + c) * ffn_rows, ffn_rows, 0),
            BOTH,
            axis=0,
            tiled=True,
        )
        for c in range(CHUNKS)
    ]
    index = jnp.arange(token_rows, dtype=jnp.int32)
    valid = (index < counts[0]).astype(jnp.float32)[:, None]
    allowed = (index[None, :] <= index[:, None]) & (index[None, :] >= (index - positions)[:, None])
    gain_one = full_gains[0].astype(jnp.float32)
    gain_two = full_gains[1].astype(jnp.float32)
    query_gain = full_qk[0].astype(jnp.float32)
    k_gain = full_qk[1].astype(jnp.float32)
    wide = tokens.astype(jnp.float32)
    inv_one = lax.rsqrt(jnp.mean(wide * wide, axis=-1, keepdims=True) + EPS)
    unit_one = wide * inv_one
    normed_one = (unit_one * gain_one).astype(jnp.bfloat16)
    projected_output = jnp.dot(normed_one, full_attn[:, :width], preferred_element_type=jnp.float32)
    query = projected_output[:, :QUERY_FEATURES].reshape(token_rows, QUERY_HEADS, HEAD_WIDTH)
    key_rows = projected_output[:, QUERY_FEATURES : QUERY_FEATURES + KEY_FEATURES].reshape(
        token_rows, KEY_VALUE_HEADS, HEAD_WIDTH
    )
    value_rows = (
        projected_output[:, QUERY_FEATURES + KEY_FEATURES :]
        .reshape(token_rows, KEY_VALUE_HEADS, HEAD_WIDTH)
        .astype(jnp.bfloat16)
    )
    q_inv = lax.rsqrt(jnp.mean(query * query, axis=-1, keepdims=True) + EPS)
    query_unit = query * q_inv
    k_inv = lax.rsqrt(jnp.mean(key_rows * key_rows, axis=-1, keepdims=True) + EPS)
    k_unit = key_rows * k_inv
    cosine_table, sine_table = rope_tables(positions, HEAD_WIDTH)
    query_rotated = (
        apply_rotation(query_unit * query_gain, cosine_table, sine_table, 1.0)
        .astype(jnp.bfloat16)
        .reshape(token_rows, KEY_VALUE_HEADS, replica_group, HEAD_WIDTH)
    )
    key_r = apply_rotation(k_unit * k_gain, cosine_table, sine_table, 1.0).astype(jnp.bfloat16)
    scores = (
        jnp.einsum("qhgd,khd->hgqk", query_rotated, key_r, preferred_element_type=jnp.float32)
        * scale
    )
    masked = jnp.where(allowed, scores, -1e30)
    top = jnp.max(masked, axis=-1, keepdims=True)
    lse = top + jnp.log(jnp.sum(jnp.exp(masked - top), axis=-1, keepdims=True))
    probs = jnp.exp(masked - lse).astype(jnp.bfloat16)
    attended = jnp.einsum(
        "hgqk,khd->qhgd", probs, value_rows, preferred_element_type=jnp.float32
    ).astype(jnp.bfloat16)
    attended_flat = attended.reshape(token_rows, QUERY_FEATURES)
    mid = wide + times_trans(attended_flat, full_attn[:, width:])
    inv_two = lax.rsqrt(jnp.mean(mid * mid, axis=-1, keepdims=True) + EPS)
    unit_two = mid * inv_two
    normed_two = (unit_two * gain_two).astype(jnp.bfloat16)
    cot = (cotangent.astype(jnp.float32) * valid).astype(jnp.bfloat16)
    total = 0.0
    d_normed = 0.0
    ffn_terms = []
    for piece in pieces:
        gate = times_trans(normed_two, piece[:, 0, :])
        up_proj = times_trans(normed_two, piece[:, 1, :])
        d_hidden = times_trans(cot, piece[:, 2, :])
        sig = jax.nn.sigmoid(gate)
        act = gate * sig
        hidden_piece = (act * up_proj).astype(jnp.bfloat16)
        d_gate = (d_hidden * up_proj * sig * (1.0 + gate * (1.0 - sig))).astype(jnp.bfloat16)
        d_up = (d_hidden * act).astype(jnp.bfloat16)
        columns = [
            h.reshape(token_rows, reps * shards // 2, 2, ffn_rows)
            for h in (d_gate, d_up, hidden_piece)
        ]

        def terms_of(which):
            halves = [
                lax.dynamic_index_in_dim(h, which, 2, keepdims=False).reshape(token_rows, -1)
                for h in columns
            ]
            return [
                trans_times(h, other) for h, other in zip(halves, (normed_two, normed_two, cot))
            ]

        sent = [t.astype(jnp.bfloat16) for t in terms_of(1 - core)]
        arrived = [swap_cores(t, reps * shards) for t in sent]
        kept = [
            (t + a.astype(jnp.float32)).astype(jnp.bfloat16)
            for t, a in zip(terms_of(core), arrived)
        ]
        ffn_terms.append(scatter_cores(jnp.stack(kept, axis=1), reps * shards))
        total = total + jnp.dot(hidden_piece, piece[:, 2, :], preferred_element_type=jnp.float32)
        d_normed = (
            d_normed
            + jnp.dot(d_gate, piece[:, 0, :], preferred_element_type=jnp.float32)
            + jnp.dot(d_up, piece[:, 1, :], preferred_element_type=jnp.float32)
        )
    result = ((mid + total) * valid).astype(jnp.bfloat16)
    grad_two = jnp.sum(d_normed * unit_two, axis=0)
    d_mid = cot.astype(jnp.float32) + rms_back(d_normed, unit_two, inv_two, gain_two)
    d_mid_b = d_mid.astype(jnp.bfloat16)
    attended_gradient = jnp.dot(
        d_mid_b, full_attn[:, width:], preferred_element_type=jnp.float32
    ).astype(jnp.bfloat16)
    attention_gradient = attended_gradient.reshape(
        token_rows, KEY_VALUE_HEADS, replica_group, HEAD_WIDTH
    )
    scores_again = (
        jnp.einsum("qhgd,khd->hgqk", query_rotated, key_r, preferred_element_type=jnp.float32)
        * scale
    )
    probs_wide = jnp.exp(jnp.where(allowed, scores_again, -1e30) - lse)
    d_probs = jnp.einsum(
        "qhgd,khd->hgqk", attention_gradient, value_rows, preferred_element_type=jnp.float32
    )
    delta = jnp.sum(attention_gradient.astype(jnp.float32) * attended.astype(jnp.float32), axis=-1)
    delta = jnp.transpose(delta, (1, 2, 0))[..., None]
    d_scores = (probs_wide * (d_probs - delta) * scale).astype(jnp.bfloat16)
    d_query_r = jnp.einsum(
        "hgqk,khd->qhgd", d_scores, key_r, preferred_element_type=jnp.float32
    ).reshape(token_rows, QUERY_HEADS, HEAD_WIDTH)
    d_key_r = jnp.einsum(
        "hgqk,qhgd->khd", d_scores, query_rotated, preferred_element_type=jnp.float32
    )
    d_value = jnp.einsum(
        "hgqk,qhgd->khd", probs, attention_gradient, preferred_element_type=jnp.float32
    )
    d_q_scaled = apply_rotation(d_query_r, cosine_table, sine_table, -1.0)
    d_k_scaled = apply_rotation(d_key_r, cosine_table, sine_table, -1.0)
    grad_q = jnp.sum(d_q_scaled * query_unit, axis=(0, 1))
    grad_k = jnp.sum(d_k_scaled * k_unit, axis=(0, 1))
    d_query = rms_back(d_q_scaled, query_unit, q_inv, query_gain)
    d_key = rms_back(d_k_scaled, k_unit, k_inv, k_gain)
    d_projected = jnp.concatenate(
        [
            d_query.reshape(token_rows, QUERY_FEATURES),
            d_key.reshape(token_rows, KEY_FEATURES),
            d_value.reshape(token_rows, KEY_FEATURES),
        ],
        axis=1,
    ).astype(jnp.bfloat16)
    d_normed_one = times_trans(d_projected, full_attn[:, :width])
    grad_one = jnp.sum(d_normed_one * unit_one, axis=0)
    grad_input = (d_mid + rms_back(d_normed_one, unit_one, inv_one, gain_one)).astype(jnp.bfloat16)
    attn_terms = jnp.concatenate(
        [
            trans_times(normed_one, d_projected).astype(jnp.bfloat16),
            trans_times(d_mid_b, attended_flat).astype(jnp.bfloat16),
        ],
        axis=1,
    ).reshape(shards // 2, 2, reps, attn_rows, attn_cols)

    def attn_half(which):
        half = lax.dynamic_index_in_dim(attn_terms, which, 1, keepdims=False)
        return half.transpose(1, 0, 2, 3).reshape(-1, attn_cols)

    attn_kept = (
        attn_half(core).astype(jnp.float32)
        + swap_cores(attn_half(1 - core), reps * shards).astype(jnp.float32)
    ).astype(jnp.bfloat16)
    small = jnp.concatenate(
        [jnp.stack([grad_one, grad_two]), jnp.stack([grad_q, grad_k])], axis=1
    )
    attn_kept, small, ffn_terms = lax.optimization_barrier((attn_kept, small, ffn_terms))
    grad_attn = scatter_cores(attn_kept, reps * shards)
    grad_ffn = lax.all_gather(
        jnp.concatenate(ffn_terms, axis=0), "rep", axis=0, tiled=True
    ).astype(jnp.float32)
    grad_attn = lax.all_gather(grad_attn, "rep", axis=0, tiled=True).astype(jnp.float32)
    small = lax.psum(small, BOTH)
    grad_gains = lax.dynamic_slice_in_dim(small, member * gain_cols, gain_cols, 1)
    grad_qk = lax.dynamic_slice_in_dim(small, QUERY_FEATURES + member * qk_cols, qk_cols, 1)
    return (result, grad_input, grad_attn, grad_ffn, grad_gains, grad_qk)


def solution(mesh):
    in_specs = (
        P(("rep", "shard"), None),
        P(("rep", "shard"), None),
        P(("rep", "shard")),
        P(("rep", "shard")),
        P("shard", None),
        P("shard", None, None),
        P(None, "shard"),
        P(None, "shard"),
    )
    out_specs = (
        P(("rep", "shard"), None),
        P(("rep", "shard"), None),
        P("shard", None),
        P("shard", None, None),
        P(None, "shard"),
        P(None, "shard"),
    )
    return jax.shard_map(local, mesh=mesh, in_specs=in_specs, out_specs=out_specs, check_vma=False)
```
